128 devices in a mesh: grp: 8 (over y, core), dev: 16 (over z, x).
Axes of the slice: x: 4, y: 4, z: 4, core: 2. Of those that a mesh axis runs over, the one named last changes fastest.
Arguments:
- basis_old: float32 [128, 2097152], P(None, ('grp', 'dev')), as said below
- values_old: float32 [128], replicated, may hold values from 1 to 4
- snapshots: float32 [2, 64, 2097152], P(None, None, ('grp', 'dev'))
- wet_counts: int32 [128], P(('grp', 'dev')), may hold values from 1 to 128, as said below
Outputs:
- basis_new: float32 [128, 2097152], P(None, ('grp', 'dev'))
- values_new: float32 [128], replicated
The draws below stay inside these ranges and needn't reach their ends.
Inputs may be any that keep to these rules, and one draw needn't show every extreme that they name: `wet_counts`: every device has at least one wet block, and some device has all 128 blocks wet. basis_old is zero on every cell that wet_mask marks dry.
All inputs are finite; a program needn't handle non-finite values.
Results may differ from the reference program's by a relative error of at most 0.0003.
Values sent between devices are 32-bit elements; how exact they have to be, the bound alone decides.
No kernel may reach another device: no remote copies, remote signals or barrier semaphores. Data moves between devices by JAX's collectives and lax.ppermute only.
A program may use at most 128 MiB of HBM per device.

```python
import math
import jax
import jax.numpy as jnp
from jax import lax

K = 128
B = 64
BLOCK = 128
BLK_DEV = 128
ROWS_DEV = 16384
SHARDS = 128
ROWS = 2097152
UPDATES = 2
SWEEPS = 3


def shared_modes(key):
    return jax.random.normal(jax.random.fold_in(key, 11), (K, ROWS), jnp.float32)


def shared_counts(key):
    counts = jax.random.randint(jax.random.fold_in(key, 31), (SHARDS,), 1, BLK_DEV + 1, jnp.int32)
    chosen = jax.random.randint(jax.random.fold_in(key, 32), (), 0, SHARDS, jnp.int32)
    return counts.at[chosen].set(BLK_DEV)


def shared_mask(key):
    counts = shared_counts(key)
    cells = jnp.arange(ROWS, dtype=jnp.int32)
    owners = (cells // ROWS_DEV).astype(jnp.int32)
    blocks = (cells % ROWS_DEV // BLOCK).astype(jnp.int32)
    return (blocks < jnp.take(counts, owners)).astype(jnp.float32)


def draw_basis_old(key, part):
    return shared_modes(key) * shared_mask(key)[None, :]


def draw_snapshots(key, part):
    modes = shared_modes(key)
    coeff = jax.random.normal(jax.random.fold_in(key, 21), (UPDATES, K, B), jnp.float32)
    mode_scale = jnp.exp(jax.random.uniform(jax.random.fold_in(key, 22), (1, K, 1), jnp.float32, math.log(0.3), math.log(3.0)))
    coeff = coeff * mode_scale
    signal = jnp.einsum('ukb,km->ubm', coeff, modes)
    col_scale = jnp.exp(jax.random.uniform(jax.random.fold_in(key, 25), (UPDATES, B, 1), jnp.float32, 0.0, math.log(3.0)))
    noise = jax.random.normal(jax.random.fold_in(key, 24), (UPDATES, B, ROWS), jnp.float32)
    row_scale = jnp.exp(jax.random.uniform(jax.random.fold_in(key, 23), (ROWS,), jnp.float32, 0.0, math.log(10.0)))
    return (signal + 0.5 * noise * row_scale[None, None, :]) * col_scale


def draw_wet_counts(key, part):
    return shared_counts(key)


def setup_inputs(seed: int = 0) -> dict:
    key_of = jax.random.split(jax.random.key(seed), 5)
    return {
        "basis_old": draw_basis_old(jax.random.fold_in(key_of[4], 71), 0),
        "values_old": jnp.clip(jnp.exp(jax.random.uniform(key_of[1], (K,), jnp.float32, math.log(1.0), math.log(4.0))), 1.0, 4.0),
        "snapshots": draw_snapshots(jax.random.fold_in(key_of[4], 71), 0),
        "wet_counts": draw_wet_counts(jax.random.fold_in(key_of[4], 71), 0),
    }


def matmul_nn(left_op, right_op):
    return jnp.dot(left_op.astype(jnp.float32), right_op.astype(jnp.float32), precision=lax.Precision.HIGHEST, preferred_element_type=jnp.float32)

def matmul_nt(left_op, right_op):
    return lax.dot_general(left_op.astype(jnp.float32), right_op.astype(jnp.float32), (((1,), (1,)), ((), ())), precision=lax.Precision.HIGHEST, preferred_element_type=jnp.float32)

def matmul_tn(left_op, right_op):
    return lax.dot_general(left_op.astype(jnp.float32), right_op.astype(jnp.float32), (((0,), (0,)), ((), ())), precision=lax.Precision.HIGHEST, preferred_element_type=jnp.float32)

def assemble(values, project, factor):
    upper_block = jnp.concatenate([jnp.diag(values), project], 1)
    bottom = jnp.concatenate([jnp.zeros((factor.shape[0], values.shape[0]), jnp.float32), factor.T], 1)
    return jnp.concatenate([upper_block, bottom], 0)

def refine(core_matrix, rank_width):
    frame_now = jnp.eye(core_matrix.shape[0], rank_width, dtype=jnp.float32)
    for repeat in range(SWEEPS):
        grown_cols = matmul_nn(core_matrix, matmul_tn(core_matrix, frame_now))
        lower_part = jnp.linalg.cholesky(matmul_tn(grown_cols, grown_cols))
        frame_now = jax.scipy.linalg.solve_triangular(lower_part, grown_cols.T, lower=True).T
    return frame_now

def reference(basis_old, values_old, snapshots, wet_counts):
    cells = jnp.arange(ROWS, dtype=jnp.int32)
    owners = (cells // ROWS_DEV).astype(jnp.int32)
    blocks = (cells % ROWS_DEV // BLOCK).astype(jnp.int32)
    wet_mask = (blocks < jnp.take(wet_counts, owners)).astype(jnp.float32)
    wet_total = jnp.sum(wet_counts).astype(jnp.float32) * BLOCK
    rank_width = basis_old.shape[0]

    def update_one(state_pair, snapshot):
        current, values = state_pair
        columns = snapshot * wet_mask[None, :]
        project = matmul_nt(current, columns) / wet_total
        remainder = columns - matmul_tn(project, current)
        gram = matmul_nt(remainder, remainder) / wet_total
        factor = jnp.linalg.cholesky(gram)
        fresh_rows = jax.scipy.linalg.solve_triangular(factor, remainder, lower=True)
        core_matrix = assemble(values, project, factor)
        frame_now = refine(core_matrix, rank_width)
        stacked = jnp.concatenate([current, fresh_rows], 0)
        new_basis = matmul_tn(frame_now, stacked)
        rotated = matmul_tn(frame_now, core_matrix)
        new_values = jnp.sqrt(lax.optimization_barrier(jnp.sum(rotated * rotated, axis=1)))
        return ((new_basis, new_values), None)
    (current, values), _ = lax.scan(update_one, (basis_old, values_old), snapshots)
    return (current, values)
```

```python
import functools

import jax
import jax.numpy as jnp
from jax import lax
from jax.experimental import pallas as pl
from jax.experimental.pallas import tpu as pltpu
from jax.sharding import PartitionSpec as P

BLOCK = 128
SWEEPS = 3
MODES = 128
CHUNK = 2048
F32 = jnp.float32
BF16 = jnp.bfloat16
HIGHEST = lax.Precision.HIGHEST


def dot_nn(left_op, right_op, precision=None):
    return lax.dot_general(
        left_op, right_op, (((1,), (0,)), ((), ())), precision=precision, preferred_element_type=F32
    )


def dot_nt(left_op, right_op, precision=None):
    return lax.dot_general(
        left_op, right_op, (((1,), (1,)), ((), ())), precision=precision, preferred_element_type=F32
    )


def load_split(step, wet, basis_ref, snap_ref):
    width = basis_ref.shape[1]
    cell = lax.broadcasted_iota(jnp.int32, snap_ref.shape, 1) + step * width
    columns = jnp.where(cell < wet * BLOCK, snap_ref[...], 0.0)
    rows = jnp.concatenate([basis_ref[...], columns], 0)
    lead = rows.astype(BF16)
    rest = (rows - lead.astype(F32)).astype(BF16)
    return lead, rest


def gram_kernel(info_ref, basis_ref, snap_ref, mine_ref, other_ref, even_acc, cross_acc):
    step = pl.program_id(0)

    @pl.when(step == 0)
    def _():
        even_acc[...] = jnp.zeros_like(even_acc)
        cross_acc[...] = jnp.zeros_like(cross_acc)

    lead, rest = load_split(step, info_ref[0], basis_ref, snap_ref)
    even_acc[...] += dot_nt(lead, lead) + dot_nt(rest, rest)
    cross_acc[...] += dot_nt(lead, rest)

    @pl.when(step == pl.num_programs(0) - 1)
    def _():
        cross = cross_acc[...]
        gram = even_acc[...] + (cross + cross.T)
        row = lax.broadcasted_iota(jnp.int32, (MODES, MODES), 0)
        lane = lax.broadcasted_iota(jnp.int32, (MODES, MODES), 1)
        snap_gram = gram[MODES:, MODES:]
        diagonal = jnp.sum(jnp.where(row == lane, snap_gram, 0.0), 0, keepdims=True)
        extra = jnp.where(
            lax.broadcasted_iota(jnp.int32, (8, MODES), 0) == 0,
            jnp.broadcast_to(diagonal, (8, MODES)),
            jnp.full((8, MODES), info_ref[0].astype(F32)),
        )
        symmetric = jnp.concatenate(
            [jnp.where(lane <= row, gram[:MODES, :MODES], snap_gram), extra], 0
        )
        mixed = jnp.concatenate([gram[:MODES, MODES:], jnp.zeros((8, MODES), F32)], 0)
        first = info_ref[1] == 0
        mine_ref[...] = jnp.where(first, symmetric, mixed)
        other_ref[...] = jnp.where(first, mixed, symmetric)


def lane_of(tile, index):
    return jnp.broadcast_to(tile[:, index : index + 1], tile.shape)


def row_of(tile, index):
    return jnp.broadcast_to(tile[index : index + 1, :], tile.shape)


def tree_sum(terms):
    while len(terms) > 1:
        terms = [
            terms[i] + terms[i + 1] if i + 1 < len(terms) else terms[i]
            for i in range(0, len(terms), 2)
        ]
    return terms[0]


def inverse_factor(tiles, base):
    sub = lax.broadcasted_iota(jnp.int32, (8, MODES), 0)
    lane = lax.broadcasted_iota(jnp.int32, (8, MODES), 1)
    tiles = list(tiles)
    finished = []
    for block in range(len(tiles)):
        start = base + 8 * block
        tile = tiles[block]
        cols = [lane_of(tile, start + j) for j in range(8)]
        pivots = None
        for k in range(8):
            pivot = row_of(cols[k], k)
            pivots = pivot if pivots is None else jnp.where(sub >= k, pivot, pivots)
            unit = jnp.where(sub == k, 1.0, 0.0)
            if k < 7:
                scale = jnp.where(sub > k, cols[k], 0.0) * (1.0 / pivot)
                for j in range(8):
                    if j != k:
                        cols[j] = cols[j] - scale * row_of(cols[j], k)
                cols[k] = unit - scale
            else:
                cols[k] = unit
        root = lax.rsqrt(pivots)
        cols = [c * root for c in cols]
        inside = (lane >= start) & (lane < start + 8)
        tile = jnp.where(inside, jnp.where(lane - start == sub, 1.0, 0.0), tile)
        done = tree_sum([cols[c] * row_of(tile, c) for c in range(8)])
        finished.append(jnp.where(lane < start + 8, done, 0.0))
        if block + 1 == len(tiles):
            break
        done_rows = [row_of(done, r) for r in range(8)]
        update = [
            tree_sum([row_of(cols[c], r) * done_rows[r] for r in range(c, 8)]) for c in range(8)
        ]
        for other in range(block + 1, len(tiles)):
            kept = jnp.where(inside, 0.0, tiles[other])
            tiles[other] = kept - tree_sum(
                [lane_of(tiles[other], start + c) * update[c] for c in range(8)]
            )
    return finished


def core_kernel(batches, parity_ref, mine_ref, other_ref, values_ref, coeff_ref, out_ref, frame, gram_buf):
    first = parity_ref[0] == 0
    mine, other = mine_ref[...], other_ref[...]
    symmetric = jnp.where(first, mine, other)
    mixed = jnp.where(first, other, mine)[:MODES]
    row = lax.broadcasted_iota(jnp.int32, (MODES, MODES), 0)
    lane = lax.broadcasted_iota(jnp.int32, (MODES, MODES), 1)
    identity = jnp.where(row == lane, 1.0, 0.0)
    wet_total = symmetric[MODES + 1 : MODES + 2, 0:1] * BLOCK
    weight = 1.0 / wet_total
    diagonal = symmetric[MODES : MODES + 1, :] * weight
    symmetric = symmetric[:MODES] * weight
    flipped = symmetric.T
    basis_gram = jnp.where(lane <= row, symmetric, flipped)
    snap_gram = jnp.where(lane > row, symmetric, jnp.where(lane == row, diagonal, flipped))
    mixed = mixed * weight
    gram_all = jnp.concatenate(
        [
            jnp.concatenate([basis_gram, mixed], 1),
            jnp.concatenate([mixed.T, snap_gram], 1),
        ],
        0,
    )
    coeff = jnp.concatenate([identity, jnp.zeros((MODES, MODES), F32)], 1)
    squares = values_ref[...] * values_ref[...]
    width = MODES // batches
    for batch in range(batches):
        chosen = (lane >= batch * width) & (lane < (batch + 1) * width)
        if batch == 0:
            project = jnp.where(chosen, mixed, 0.0)
        else:
            project = jnp.where(chosen, dot_nn(coeff, gram_all[:, MODES:], HIGHEST), 0.0)
        project_t = project.T
        own = jnp.where(chosen, identity, 0.0)
        remainder = (
            jnp.concatenate([jnp.zeros((MODES, MODES), F32), own], 1)
            - dot_nn(project_t, coeff, HIGHEST)
        )
        gram = dot_nt(dot_nn(remainder, gram_all, HIGHEST), remainder, HIGHEST)
        low = batch * width
        tiles = inverse_factor(
            [gram[low + 8 * i : low + 8 * i + 8] for i in range(width // 8)], low
        )
        blank = jnp.zeros((width, MODES), F32)
        factor_inv = jnp.concatenate(
            [blank] * batch + tiles + [blank] * (batches - 1 - batch), 0
        )
        factor_t = dot_nn(factor_inv, gram, HIGHEST)
        factor_t = jnp.where((row <= lane) & chosen, factor_t, 0.0)
        fresh = dot_nn(factor_inv, remainder, HIGHEST)
        right = jnp.concatenate([project, factor_t], 0)
        right_t = jnp.concatenate([project_t, factor_t.T], 1)
        square_row = jnp.concatenate([squares, jnp.zeros((1, MODES), F32)], 1)
        frame[...] = jnp.concatenate([identity, jnp.zeros((MODES, MODES), F32)], 1)

        def sweep(repeat, carry):
            now = frame[...]
            grown = now * square_row + dot_nn(dot_nn(now, right, HIGHEST), right_t, HIGHEST)
            square = dot_nt(grown, grown, HIGHEST)
            inverse = inverse_factor([square[8 * i : 8 * i + 8] for i in range(MODES // 8)], 0)
            frame[...] = dot_nn(jnp.concatenate(inverse, 0), grown, HIGHEST)
            return carry

        lax.fori_loop(0, SWEEPS, sweep, 0)
        now = frame[...]
        side = dot_nn(now, right, HIGHEST)
        head = now[:, :MODES]
        energy = head * head * squares + side * side
        squares = dot_nt(jnp.ones((8, MODES), F32), energy, HIGHEST)[:1]
        coeff = dot_nn(now, jnp.concatenate([coeff, fresh], 0), HIGHEST)
    lead = coeff.astype(BF16)
    rest = (coeff - lead.astype(F32)).astype(BF16)
    coeff_ref[...] = jnp.concatenate([lead, rest], 0)
    out_ref[...] = jnp.sqrt(squares)


def apply_kernel(info_ref, coeff_ref, basis_ref, snap_ref, out_ref):
    lead, rest = load_split(pl.program_id(0), info_ref[0], basis_ref, snap_ref)
    both = dot_nn(coeff_ref[...], lead)
    out_ref[...] = (both[:MODES] + both[MODES:]) + dot_nn(coeff_ref[:MODES, :], rest)


def exchange(array, axis, move):
    size = lax.axis_size(axis)
    return lax.ppermute(array, axis, [(i, move(i)) for i in range(size)])


def ring_step(axis, stride, hop):
    def move(i):
        place = (i // stride) % 4
        return i + ((place + hop) % 4 - place) * stride

    return functools.partial(exchange, axis=axis, move=move)


def total_over_devices(mine, other):
    part = mine + exchange(other, "grp", lambda i: i ^ 1)
    for axis, stride in (("grp", 2), ("dev", 1), ("dev", 4)):
        part = (part + ring_step(axis, stride, 2)(part)) + (
            ring_step(axis, stride, 1)(part) + ring_step(axis, stride, 3)(part)
        )
    return part, exchange(part, "grp", lambda i: i ^ 1)


def per_device(basis_old, values_old, snapshots, wet_counts):
    batches, batch_width, cells = snapshots.shape
    snaps = snapshots.reshape(batches * batch_width, cells)
    parity = (lax.axis_index("grp") % 2).astype(jnp.int32)
    info = jnp.stack([wet_counts[0], parity])
    smem = pl.BlockSpec(memory_space=pltpu.SMEM)
    grid = (cells // CHUNK,)
    stream = pl.BlockSpec((MODES, CHUNK), lambda i: (0, i))
    half = jax.ShapeDtypeStruct((MODES + 8, MODES), F32)
    whole = pl.BlockSpec((MODES + 8, MODES), lambda i: (0, 0))
    mine, other = pl.pallas_call(
        gram_kernel,
        grid=grid,
        in_specs=[smem, stream, stream],
        out_specs=[whole, whole],
        out_shape=[half, half],
        scratch_shapes=[pltpu.VMEM((2 * MODES, 2 * MODES), F32)] * 2,
        name="gram",
    )(info, basis_old, snaps)
    mine, other = total_over_devices(mine, other)
    coeff, values = pl.pallas_call(
        functools.partial(core_kernel, batches),
        in_specs=[smem] + [pl.BlockSpec(memory_space=pltpu.VMEM)] * 3,
        out_specs=[pl.BlockSpec(memory_space=pltpu.VMEM)] * 2,
        out_shape=[
            jax.ShapeDtypeStruct((2 * MODES, 2 * MODES), BF16),
            jax.ShapeDtypeStruct((1, MODES), F32),
        ],
        scratch_shapes=[
            pltpu.VMEM((MODES, 2 * MODES), F32),
            pltpu.VMEM((MODES, MODES), F32),
        ],
        name="core",
    )(parity[None], mine, other, values_old[None, :])
    basis = pl.pallas_call(
        apply_kernel,
        grid=grid,
        in_specs=[smem, pl.BlockSpec((2 * MODES, 2 * MODES), lambda i: (0, 0)), stream, stream],
        out_specs=stream,
        out_shape=jax.ShapeDtypeStruct((MODES, cells), F32),
        name="apply",
    )(info, coeff, basis_old, snaps)
    return basis, values[0]


def solution(mesh):
    return jax.shard_map(
        per_device,
        mesh=mesh,
        in_specs=(P(None, ("grp", "dev")), P(), P(None, None, ("grp", "dev")), P(("grp", "dev"))),
        out_specs=(P(None, ("grp", "dev")), P()),
        check_vma=False,
    )
```

```python
import functools

import jax
import jax.numpy as jnp
from jax import lax
from jax.experimental import pallas as pl
from jax.experimental.pallas import tpu as pltpu
from jax.sharding import PartitionSpec as P

BLOCK = 128
SWEEPS = 3
MODES = 128
GRAM_PARTS = 8
APPLY_PARTS = 16
GRAM_VMEM = 8 << 20
CORE_VMEM = 8 << 20
APPLY_VMEM = 14 << 20
F32 = jnp.float32
BF16 = jnp.bfloat16
HIGHEST = lax.Precision.HIGHEST


def dot_nn(left_op, right_op, precision=None):
    return lax.dot_general(
        left_op, right_op, (((1,), (0,)), ((), ())), precision=precision, preferred_element_type=F32
    )


def dot_nt(left_op, right_op, precision=None):
    return lax.dot_general(
        left_op, right_op, (((1,), (1,)), ((), ())), precision=precision, preferred_element_type=F32
    )


def split_rows(basis, snap, start, wet):
    cell = lax.broadcasted_iota(jnp.int32, snap.shape, 1) + start
    snap = jnp.where(cell < wet * BLOCK, snap, 0.0)
    basis_lead, snap_lead = basis.astype(BF16), snap.astype(BF16)
    basis_rest = (basis - basis_lead.astype(F32)).astype(BF16)
    snap_rest = (snap - snap_lead.astype(F32)).astype(BF16)
    return (
        jnp.concatenate([basis_lead, snap_lead], 0),
        jnp.concatenate([basis_rest, snap_rest], 0),
    )


def gram_kernel(
    info_ref, basis_hbm, snap_hbm, mine_ref, other_ref, basis_buf, snap_buf, arrived, even_acc, cross_acc, energy
):
    width = basis_hbm.shape[1] // GRAM_PARTS
    copies = []
    for part in range(GRAM_PARTS):
        span = pl.ds(part * width, width)
        copies.append(
            [
                pltpu.make_async_copy(source.at[:, span], target.at[:, span], arrived.at[which, part])
                for which, (source, target) in enumerate(
                    [(basis_hbm, basis_buf), (snap_hbm, snap_buf)]
                )
            ]
        )
        for copy in copies[-1]:
            copy.start()
    for part in range(GRAM_PARTS):
        for copy in copies[part]:
            copy.wait()
        span = pl.ds(part * width, width)
        lead, rest = split_rows(basis_buf[:, span], snap_buf[:, span], part * width, info_ref[0])
        step, mixed_step = dot_nt(lead, lead), dot_nt(rest, lead)
        square = rest.astype(F32)
        square = square * square
        folded = square[:, :BLOCK]
        for k in range(1, width // BLOCK):
            folded = folded + square[:, k * BLOCK : (k + 1) * BLOCK]
        even_acc[...] = step if part == 0 else even_acc[...] + step
        cross_acc[...] = mixed_step if part == 0 else cross_acc[...] + mixed_step
        energy[...] = folded if part == 0 else energy[...] + folded

    row = lax.broadcasted_iota(jnp.int32, (MODES, MODES), 0)
    lane = lax.broadcasted_iota(jnp.int32, (MODES, MODES), 1)
    cross = cross_acc[...]
    gram = even_acc[...] + (cross + cross.T)
    extra_basis = jnp.sum(energy[:MODES, :], 1, keepdims=True)
    extra_snap = jnp.sum(energy[MODES:, :], 1, keepdims=True)
    basis_gram = gram[:MODES, :MODES] + jnp.where(row == lane, extra_basis, 0.0)
    snap_gram = gram[MODES:, MODES:]
    diagonal = jnp.sum(jnp.where(row == lane, snap_gram + extra_snap, 0.0), 0, keepdims=True)
    extra = jnp.where(
        lax.broadcasted_iota(jnp.int32, (8, MODES), 0) == 0,
        jnp.broadcast_to(diagonal, (8, MODES)),
        jnp.full((8, MODES), info_ref[0].astype(F32)),
    )
    symmetric = jnp.concatenate([jnp.where(lane <= row, basis_gram, snap_gram), extra], 0)
    mixed = jnp.concatenate([gram[:MODES, MODES:], jnp.zeros((8, MODES), F32)], 0)
    first = info_ref[1] == 0
    mine_ref[...] = jnp.where(first, symmetric, mixed)
    other_ref[...] = jnp.where(first, mixed, symmetric)


def lane_of(tile, index):
    return jnp.broadcast_to(tile[:, index : index + 1], tile.shape)


def row_of(tile, index):
    return jnp.broadcast_to(tile[index : index + 1, :], tile.shape)


def tree_sum(terms):
    while len(terms) > 1:
        terms = [
            terms[i] + terms[i + 1] if i + 1 < len(terms) else terms[i]
            for i in range(0, len(terms), 2)
        ]
    return terms[0]


def inverse_factor(tiles, base):
    sub = lax.broadcasted_iota(jnp.int32, (8, MODES), 0)
    lane = lax.broadcasted_iota(jnp.int32, (8, MODES), 1)
    tiles = list(tiles)
    finished = []
    for block in range(len(tiles)):
        start = base + 8 * block
        tile = tiles[block]
        cols = [lane_of(tile, start + j) for j in range(8)]
        pivots = None
        for k in range(8):
            pivot = row_of(cols[k], k)
            pivots = pivot if pivots is None else jnp.where(sub >= k, pivot, pivots)
            unit = jnp.where(sub == k, 1.0, 0.0)
            if k < 7:
                scale = jnp.where(sub > k, cols[k], 0.0) * (1.0 / pivot)
                for j in range(8):
                    if j != k:
                        cols[j] = cols[j] - scale * row_of(cols[j], k)
                cols[k] = unit - scale
            else:
                cols[k] = unit
        root = lax.rsqrt(pivots)
        cols = [c * root for c in cols]
        inside = (lane >= start) & (lane < start + 8)
        tile = jnp.where(inside, jnp.where(lane - start == sub, 1.0, 0.0), tile)
        done = tree_sum([cols[c] * row_of(tile, c) for c in range(8)])
        finished.append(jnp.where(lane < start + 8, done, 0.0))
        if block + 1 == len(tiles):
            break
        done_rows = [row_of(done, r) for r in range(8)]
        update = [
            tree_sum([row_of(cols[c], r) * done_rows[r] for r in range(c, 8)]) for c in range(8)
        ]
        for other in range(block + 1, len(tiles)):
            kept = jnp.where(inside, 0.0, tiles[other])
            tiles[other] = kept - tree_sum(
                [lane_of(tiles[other], start + c) * update[c] for c in range(8)]
            )
    return finished


def core_kernel(batches, parity_ref, mine_ref, other_ref, values_ref, coeff_ref, out_ref, frame, grown_buf):
    first = parity_ref[0] == 0
    mine, other = mine_ref[...], other_ref[...]
    symmetric = jnp.where(first, mine, other)
    mixed = jnp.where(first, other, mine)[:MODES]
    row = lax.broadcasted_iota(jnp.int32, (MODES, MODES), 0)
    lane = lax.broadcasted_iota(jnp.int32, (MODES, MODES), 1)
    identity = jnp.where(row == lane, 1.0, 0.0)
    wet_total = symmetric[MODES + 1 : MODES + 2, 0:1] * BLOCK
    weight = 1.0 / wet_total
    diagonal = symmetric[MODES : MODES + 1, :] * weight
    symmetric = symmetric[:MODES] * weight
    flipped = symmetric.T
    basis_gram = jnp.where(lane <= row, symmetric, flipped)
    snap_gram = jnp.where(lane > row, symmetric, jnp.where(lane == row, diagonal, flipped))
    mixed = mixed * weight
    gram_all = jnp.concatenate(
        [
            jnp.concatenate([basis_gram, mixed], 1),
            jnp.concatenate([mixed.T, snap_gram], 1),
        ],
        0,
    )
    coeff = jnp.concatenate([identity, jnp.zeros((MODES, MODES), F32)], 1)
    squares = values_ref[...] * values_ref[...]
    width = MODES // batches
    for batch in range(batches):
        chosen = (lane >= batch * width) & (lane < (batch + 1) * width)
        if batch == 0:
            project = jnp.where(chosen, mixed, 0.0)
        else:
            project = jnp.where(chosen, dot_nn(coeff, gram_all[:, MODES:], HIGHEST), 0.0)
        project_t = project.T
        own = jnp.where(chosen, identity, 0.0)
        remainder = (
            jnp.concatenate([jnp.zeros((MODES, MODES), F32), own], 1)
            - dot_nn(project_t, coeff, HIGHEST)
        )
        gram = dot_nt(dot_nn(remainder, gram_all, HIGHEST), remainder, HIGHEST)
        low = batch * width
        tiles = inverse_factor(
            [gram[low + 8 * i : low + 8 * i + 8] for i in range(width // 8)], low
        )
        blank = jnp.zeros((width, MODES), F32)
        factor_inv = jnp.concatenate(
            [blank] * batch + tiles + [blank] * (batches - 1 - batch), 0
        )
        factor_t = dot_nn(factor_inv, gram, HIGHEST)
        factor_t = jnp.where((row <= lane) & chosen, factor_t, 0.0)
        fresh = dot_nn(factor_inv, remainder, HIGHEST)
        right = jnp.concatenate([project, factor_t], 0)
        right_t = jnp.concatenate([project_t, factor_t.T], 1)
        square_row = jnp.concatenate([squares, jnp.zeros((1, MODES), F32)], 1)
        frame[...] = jnp.concatenate([identity, jnp.zeros((MODES, MODES), F32)], 1)

        def sweep(repeat, carry):
            now = frame[...]
            grown = now * square_row + dot_nn(dot_nn(now, right, HIGHEST), right_t, HIGHEST)
            square = dot_nt(grown, grown, HIGHEST)
            inverse = inverse_factor([square[8 * i : 8 * i + 8] for i in range(MODES // 8)], 0)
            frame[...] = dot_nn(jnp.concatenate(inverse, 0), grown, HIGHEST)
            return carry

        lax.fori_loop(0, SWEEPS, sweep, 0)
        now = frame[...]
        side = dot_nn(now, right, HIGHEST)
        head = now[:, :MODES]
        energy = head * head * squares + side * side
        squares = dot_nt(jnp.ones((8, MODES), F32), energy, HIGHEST)[:1]
        coeff = dot_nn(now, jnp.concatenate([coeff, fresh], 0), HIGHEST)
    lead = coeff.astype(BF16)
    rest = (coeff - lead.astype(F32)).astype(BF16)
    coeff_ref[...] = jnp.concatenate([lead, rest], 0)
    out_ref[...] = jnp.sqrt(squares)


def apply_kernel(info_ref, coeff_ref, basis_ref, snap_ref, out_hbm, buffer, sent):
    width = out_hbm.shape[1] // APPLY_PARTS
    copies = []
    for part in range(APPLY_PARTS):
        span = pl.ds(part * width, width)
        lead, rest = split_rows(basis_ref[:, span], snap_ref[:, span], part * width, info_ref[0])
        both = dot_nn(coeff_ref[...], lead)
        buffer[:, span] = (both[:MODES] + both[MODES:]) + dot_nn(coeff_ref[:MODES, :], rest)
        copies.append(
            pltpu.make_async_copy(buffer.at[:, span], out_hbm.at[:, span], sent.at[part])
        )
        copies[-1].start()
    for copy in copies:
        copy.wait()


def exchange(array, axis, move):
    size = lax.axis_size(axis)
    return lax.ppermute(array, axis, [(i, move(i)) for i in range(size)])


def ring_step(axis, stride, hop):
    def move(i):
        place = (i // stride) % 4
        return i + ((place + hop) % 4 - place) * stride

    return functools.partial(exchange, axis=axis, move=move)


def total_over_devices(mine, other):
    part = mine + exchange(other, "grp", lambda i: i ^ 1)
    for axis, stride in (("grp", 2), ("dev", 1), ("dev", 4)):
        part = (part + ring_step(axis, stride, 2)(part)) + (
            ring_step(axis, stride, 1)(part) + ring_step(axis, stride, 3)(part)
        )
    return part, exchange(part, "grp", lambda i: i ^ 1)


VMEM = pl.BlockSpec(memory_space=pltpu.VMEM)
SMEM = pl.BlockSpec(memory_space=pltpu.SMEM)
ANYWHERE = pl.BlockSpec(memory_space=pl.ANY)


def gram_call(info, basis, snaps):
    cells = basis.shape[1]
    half = jax.ShapeDtypeStruct((MODES + 8, MODES), F32)
    near = jax.ShapeDtypeStruct((MODES, cells), F32)
    return pl.pallas_call(
        gram_kernel,
        in_specs=[SMEM, ANYWHERE, ANYWHERE],
        out_specs=[VMEM] * 4,
        out_shape=[half, half, near, near],
        scratch_shapes=[
            pltpu.SemaphoreType.DMA((2, GRAM_PARTS)),
            pltpu.VMEM((2 * MODES, 2 * MODES), F32),
            pltpu.VMEM((2 * MODES, 2 * MODES), F32),
            pltpu.VMEM((2 * MODES, BLOCK), F32),
        ],
        compiler_params=pltpu.CompilerParams(vmem_limit_bytes=GRAM_VMEM),
        name="gram",
    )(info, basis, snaps)


def core_call(parity, mine, other, values, batches=2):
    return pl.pallas_call(
        functools.partial(core_kernel, batches),
        in_specs=[SMEM, VMEM, VMEM, VMEM],
        out_specs=[VMEM, VMEM],
        out_shape=[
            jax.ShapeDtypeStruct((2 * MODES, 2 * MODES), BF16),
            jax.ShapeDtypeStruct((1, MODES), F32),
        ],
        scratch_shapes=[pltpu.VMEM((MODES, 2 * MODES), F32)] * 2,
        compiler_params=pltpu.CompilerParams(vmem_limit_bytes=CORE_VMEM),
        name="core",
    )(parity, mine, other, values)


def apply_call(info, coeff, basis, snaps):
    cells = basis.shape[1]
    return pl.pallas_call(
        apply_kernel,
        in_specs=[SMEM, VMEM, VMEM, VMEM],
        out_specs=ANYWHERE,
        out_shape=jax.ShapeDtypeStruct((MODES, cells), F32),
        scratch_shapes=[
            pltpu.VMEM((MODES, cells), F32),
            pltpu.SemaphoreType.DMA((APPLY_PARTS,)),
        ],
        compiler_params=pltpu.CompilerParams(vmem_limit_bytes=APPLY_VMEM),
        name="apply",
    )(info, coeff, basis, snaps)


def per_device(basis_old, values_old, snapshots, wet_counts):
    batches, batch_width, cells = snapshots.shape
    snaps = snapshots.reshape(batches * batch_width, cells)
    parity = (lax.axis_index("grp") % 2).astype(jnp.int32)
    info = jnp.stack([wet_counts[0], parity])
    far = pltpu.with_memory_space_constraint(basis_old, pltpu.HBM)
    far_snaps = pltpu.with_memory_space_constraint(snaps, pltpu.HBM)
    mine, other, near_basis, near_snaps = gram_call(info, far, far_snaps)
    mine, other = total_over_devices(mine, other)
    coeff, values = core_call(parity[None], mine, other, values_old[None, :], batches)
    basis = apply_call(info, coeff, near_basis, near_snaps)
    return basis, values[0]


def solution(mesh):
    return jax.shard_map(
        per_device,
        mesh=mesh,
        in_specs=(P(None, ("grp", "dev")), P(), P(None, None, ("grp", "dev")), P(("grp", "dev"))),
        out_specs=(P(None, ("grp", "dev")), P()),
        check_vma=False,
    )
```

```python
import functools

import jax
import jax.numpy as jnp
from jax import lax
from jax.experimental import pallas as pl
from jax.experimental.pallas import tpu as pltpu
from jax.sharding import PartitionSpec as P

BLOCK = 128
SWEEPS = 3
MODES = 128
GRAM_PARTS = 8
APPLY_PARTS = 16
GRAM_VMEM = 8 << 20
CORE_VMEM = 8 << 20
APPLY_VMEM = 14 << 20
F32 = jnp.float32
BF16 = jnp.bfloat16
HIGHEST = lax.Precision.HIGHEST


def dot_nn(left_op, right_op, precision=None):
    return lax.dot_general(
        left_op, right_op, (((1,), (0,)), ((), ())), precision=precision, preferred_element_type=F32
    )


def dot_nt(left_op, right_op, precision=None):
    return lax.dot_general(
        left_op, right_op, (((1,), (1,)), ((), ())), precision=precision, preferred_element_type=F32
    )


def split_rows(basis, snap, start, wet):
    cell = lax.broadcasted_iota(jnp.int32, snap.shape, 1) + start
    snap = jnp.where(cell < wet * BLOCK, snap, 0.0)
    basis_lead, snap_lead = basis.astype(BF16), snap.astype(BF16)
    basis_rest = (basis - basis_lead.astype(F32)).astype(BF16)
    snap_rest = (snap - snap_lead.astype(F32)).astype(BF16)
    return (
        jnp.concatenate([basis_lead, snap_lead], 0),
        jnp.concatenate([basis_rest, snap_rest], 0),
    )


def gram_kernel(
    wet_ref, basis_hbm, snap_hbm, mine_ref, other_ref, basis_buf, snap_buf, arrived, even_acc, cross_acc, energy
):
    width = basis_hbm.shape[1] // GRAM_PARTS
    copies = []
    for part in range(GRAM_PARTS):
        span = pl.ds(part * width, width)
        copies.append(
            [
                pltpu.make_async_copy(source.at[:, span], target.at[:, span], arrived.at[which, part])
                for which, (source, target) in enumerate(
                    [(basis_hbm, basis_buf), (snap_hbm, snap_buf)]
                )
            ]
        )
        for copy in copies[-1]:
            copy.start()
    for part in range(GRAM_PARTS):
        for copy in copies[part]:
            copy.wait()
        span = pl.ds(part * width, width)
        lead, rest = split_rows(basis_buf[:, span], snap_buf[:, span], part * width, wet_ref[0])
        step, mixed_step = dot_nt(lead, lead), dot_nt(rest, lead)
        square = rest.astype(F32)
        square = square * square
        folded = square[:, :BLOCK]
        for k in range(1, width // BLOCK):
            folded = folded + square[:, k * BLOCK : (k + 1) * BLOCK]
        even_acc[...] = step if part == 0 else even_acc[...] + step
        cross_acc[...] = mixed_step if part == 0 else cross_acc[...] + mixed_step
        energy[...] = folded if part == 0 else energy[...] + folded

    row = lax.broadcasted_iota(jnp.int32, (MODES, MODES), 0)
    lane = lax.broadcasted_iota(jnp.int32, (MODES, MODES), 1)
    cross = cross_acc[...]
    gram = even_acc[...] + (cross + cross.T)
    extra_basis = jnp.sum(energy[:MODES, :], 1, keepdims=True)
    extra_snap = jnp.sum(energy[MODES:, :], 1, keepdims=True)
    basis_gram = gram[:MODES, :MODES] + jnp.where(row == lane, extra_basis, 0.0)
    snap_gram = gram[MODES:, MODES:]
    diagonal = jnp.sum(jnp.where(row == lane, snap_gram + extra_snap, 0.0), 0, keepdims=True)
    extra = jnp.where(
        lax.broadcasted_iota(jnp.int32, (8, MODES), 0) == 0,
        jnp.broadcast_to(diagonal, (8, MODES)),
        jnp.full((8, MODES), wet_ref[0].astype(F32)),
    )
    symmetric = jnp.concatenate([jnp.where(lane <= row, basis_gram, snap_gram), extra], 0)
    mixed = jnp.concatenate([gram[:MODES, MODES:], jnp.zeros((8, MODES), F32)], 0)
    first = lax.axis_index("grp") % 2 == 0
    mine_ref[...] = jnp.where(first, symmetric, mixed)
    other_ref[...] = jnp.where(first, mixed, symmetric)


def lane_of(tile, index):
    return jnp.broadcast_to(tile[:, index : index + 1], tile.shape)


def row_of(tile, index):
    return jnp.broadcast_to(tile[index : index + 1, :], tile.shape)


def tree_sum(terms):
    while len(terms) > 1:
        terms = [
            terms[i] + terms[i + 1] if i + 1 < len(terms) else terms[i]
            for i in range(0, len(terms), 2)
        ]
    return terms[0]


def factor_steps(tiles, base):
    sub = lax.broadcasted_iota(jnp.int32, (8, MODES), 0)
    lane = lax.broadcasted_iota(jnp.int32, (8, MODES), 1)
    tiles = list(tiles)
    finished = []
    for block in range(len(tiles)):
        start = base + 8 * block
        tile = tiles[block]
        cols = [lane_of(tile, start + j) for j in range(8)]
        pivots = None
        for k in range(8):
            pivot = row_of(cols[k], k)
            pivots = pivot if pivots is None else jnp.where(sub >= k, pivot, pivots)
            unit = jnp.where(sub == k, 1.0, 0.0)
            if k < 7:
                scale = jnp.where(sub > k, cols[k], 0.0) * (1.0 / pivot)
                for j in range(8):
                    if j != k:
                        cols[j] = cols[j] - scale * row_of(cols[j], k)
                cols[k] = unit - scale
            else:
                cols[k] = unit
        root = lax.rsqrt(pivots)
        cols = [c * root for c in cols]
        inside = (lane >= start) & (lane < start + 8)
        tile = jnp.where(inside, jnp.where(lane - start == sub, 1.0, 0.0), tile)
        done = tree_sum([cols[c] * row_of(tile, c) for c in range(8)])
        finished.append(jnp.where(lane < start + 8, done, 0.0))
        yield
        if block + 1 == len(tiles):
            break
        done_rows = [row_of(done, r) for r in range(8)]
        update = [
            tree_sum([row_of(cols[c], r) * done_rows[r] for r in range(c, 8)]) for c in range(8)
        ]
        for other in range(block + 1, len(tiles)):
            kept = jnp.where(inside, 0.0, tiles[other])
            tiles[other] = kept - tree_sum(
                [lane_of(tiles[other], start + c) * update[c] for c in range(8)]
            )
    return finished


def run_together(*steppers):
    results = [None] * len(steppers)
    open_ones = dict(enumerate(steppers))
    while open_ones:
        for which, stepper in list(open_ones.items()):
            try:
                next(stepper)
            except StopIteration as end:
                results[which] = end.value
                del open_ones[which]
    return results


def tiles_of(matrix, start, count):
    return [matrix[start + 8 * i : start + 8 * i + 8] for i in range(count)]


def core_kernel(batches, mine_ref, other_ref, values_ref, coeff_ref, out_ref, frame):
    first = lax.axis_index("grp") % 2 == 0
    mine, other = mine_ref[...], other_ref[...]
    symmetric = jnp.where(first, mine, other)
    mixed = jnp.where(first, other, mine)[:MODES]
    row = lax.broadcasted_iota(jnp.int32, (MODES, MODES), 0)
    lane = lax.broadcasted_iota(jnp.int32, (MODES, MODES), 1)
    identity = jnp.where(row == lane, 1.0, 0.0)
    wet_total = symmetric[MODES + 1 : MODES + 2, 0:1] * BLOCK
    weight = 1.0 / wet_total
    diagonal = symmetric[MODES : MODES + 1, :] * weight
    symmetric = symmetric[:MODES] * weight
    flipped = symmetric.T
    basis_gram = jnp.where(lane <= row, symmetric, flipped)
    snap_gram = jnp.where(lane > row, symmetric, jnp.where(lane == row, diagonal, flipped))
    mixed = mixed * weight
    gram_all = jnp.concatenate(
        [
            jnp.concatenate([basis_gram, mixed], 1),
            jnp.concatenate([mixed.T, snap_gram], 1),
        ],
        0,
    )
    coeff = jnp.concatenate([identity, jnp.zeros((MODES, MODES), F32)], 1)
    squares = values_ref[...] * values_ref[...]
    width = MODES // batches
    for batch in range(batches):
        chosen = (lane >= batch * width) & (lane < (batch + 1) * width)
        if batch == 0:
            project = jnp.where(chosen, mixed, 0.0)
        else:
            project = jnp.where(chosen, dot_nn(coeff, gram_all[:, MODES:], HIGHEST), 0.0)
        project_t = project.T
        own = jnp.where(chosen, identity, 0.0)
        remainder = (
            jnp.concatenate([jnp.zeros((MODES, MODES), F32), own], 1)
            - dot_nn(project_t, coeff, HIGHEST)
        )
        gram = dot_nt(dot_nn(remainder, gram_all, HIGHEST), remainder, HIGHEST)
        low = batch * width
        head = jnp.where(row == lane, squares, 0.0) + dot_nn(project, project_t, HIGHEST)
        square = dot_nt(head, head, HIGHEST) + dot_nt(
            dot_nn(project, gram, HIGHEST), project, HIGHEST
        )
        tiles, inverse = run_together(
            factor_steps(tiles_of(gram, low, width // 8), low),
            factor_steps(tiles_of(square, 0, MODES // 8), 0),
        )
        blank = jnp.zeros((width, MODES), F32)
        factor_inv = jnp.concatenate(
            [blank] * batch + tiles + [blank] * (batches - 1 - batch), 0
        )
        factor_t = dot_nn(factor_inv, gram, HIGHEST)
        factor_t = jnp.where((row <= lane) & chosen, factor_t, 0.0)
        factor = factor_t.T
        fresh = dot_nn(factor_inv, remainder, HIGHEST)
        right = jnp.concatenate([project, factor_t], 0)
        right_t = jnp.concatenate([project_t, factor], 1)
        square_row = jnp.concatenate([squares, jnp.zeros((1, MODES), F32)], 1)
        grown = jnp.concatenate([head, dot_nn(project, factor, HIGHEST)], 1)
        frame[...] = dot_nn(jnp.concatenate(inverse, 0), grown, HIGHEST)

        def sweep(repeat, carry):
            now = frame[...]
            grown = now * square_row + dot_nn(dot_nn(now, right, HIGHEST), right_t, HIGHEST)
            square = dot_nt(grown, grown, HIGHEST)
            (inverse,) = run_together(factor_steps(tiles_of(square, 0, MODES // 8), 0))
            frame[...] = dot_nn(jnp.concatenate(inverse, 0), grown, HIGHEST)
            return carry

        lax.fori_loop(1, SWEEPS, sweep, 0)
        now = frame[...]
        side = dot_nn(now, right, HIGHEST)
        head = now[:, :MODES]
        energy = head * head * squares + side * side
        squares = dot_nt(jnp.ones((8, MODES), F32), energy, HIGHEST)[:1]
        coeff = dot_nn(now, jnp.concatenate([coeff, fresh], 0), HIGHEST)
    lead = coeff.astype(BF16)
    rest = (coeff - lead.astype(F32)).astype(BF16)
    coeff_ref[...] = jnp.concatenate([lead, rest], 0)
    out_ref[...] = jnp.sqrt(squares)


def apply_kernel(wet_ref, coeff_ref, basis_ref, snap_ref, out_hbm, buffer, sent):
    width = out_hbm.shape[1] // APPLY_PARTS
    copies = []
    for part in range(APPLY_PARTS):
        span = pl.ds(part * width, width)
        lead, rest = split_rows(basis_ref[:, span], snap_ref[:, span], part * width, wet_ref[0])
        both = dot_nn(coeff_ref[...], lead)
        buffer[:, span] = (both[:MODES] + both[MODES:]) + dot_nn(coeff_ref[:MODES, :], rest)
        copies.append(
            pltpu.make_async_copy(buffer.at[:, span], out_hbm.at[:, span], sent.at[part])
        )
        copies[-1].start()
    for copy in copies:
        copy.wait()


def exchange(array, axis, move):
    size = lax.axis_size(axis)
    return lax.ppermute(array, axis, [(i, move(i)) for i in range(size)])


def ring_step(axis, stride, hop):
    def move(i):
        place = (i // stride) % 4
        return i + ((place + hop) % 4 - place) * stride

    return functools.partial(exchange, axis=axis, move=move)


def total_over_devices(mine, other):
    part = mine + exchange(other, "grp", lambda i: i ^ 1)
    for axis, stride in (("grp", 2), ("dev", 1), ("dev", 4)):
        part = (part + ring_step(axis, stride, 2)(part)) + (
            ring_step(axis, stride, 1)(part) + ring_step(axis, stride, 3)(part)
        )
    return part, exchange(part, "grp", lambda i: i ^ 1)


VMEM = pl.BlockSpec(memory_space=pltpu.VMEM)
SMEM = pl.BlockSpec(memory_space=pltpu.SMEM)
ANYWHERE = pl.BlockSpec(memory_space=pl.ANY)


def gram_call(wet, basis, snaps):
    cells = basis.shape[1]
    half = jax.ShapeDtypeStruct((MODES + 8, MODES), F32)
    near = jax.ShapeDtypeStruct((MODES, cells), F32)
    return pl.pallas_call(
        gram_kernel,
        in_specs=[SMEM, ANYWHERE, ANYWHERE],
        out_specs=[VMEM] * 4,
        out_shape=[half, half, near, near],
        scratch_shapes=[
            pltpu.SemaphoreType.DMA((2, GRAM_PARTS)),
            pltpu.VMEM((2 * MODES, 2 * MODES), F32),
            pltpu.VMEM((2 * MODES, 2 * MODES), F32),
            pltpu.VMEM((2 * MODES, BLOCK), F32),
        ],
        compiler_params=pltpu.CompilerParams(vmem_limit_bytes=GRAM_VMEM),
        name="gram",
    )(wet, basis, snaps)


def core_call(mine, other, values, batches=2):
    return pl.pallas_call(
        functools.partial(core_kernel, batches),
        in_specs=[VMEM, VMEM, VMEM],
        out_specs=[VMEM, VMEM],
        out_shape=[
            jax.ShapeDtypeStruct((2 * MODES, 2 * MODES), BF16),
            jax.ShapeDtypeStruct((1, MODES), F32),
        ],
        scratch_shapes=[pltpu.VMEM((MODES, 2 * MODES), F32)],
        compiler_params=pltpu.CompilerParams(vmem_limit_bytes=CORE_VMEM),
        name="core",
    )(mine, other, values)


def apply_call(wet, coeff, basis, snaps):
    cells = basis.shape[1]
    return pl.pallas_call(
        apply_kernel,
        in_specs=[SMEM, VMEM, VMEM, VMEM],
        out_specs=ANYWHERE,
        out_shape=jax.ShapeDtypeStruct((MODES, cells), F32),
        scratch_shapes=[
            pltpu.VMEM((MODES, cells), F32),
            pltpu.SemaphoreType.DMA((APPLY_PARTS,)),
        ],
        compiler_params=pltpu.CompilerParams(vmem_limit_bytes=APPLY_VMEM),
        name="apply",
    )(wet, coeff, basis, snaps)


def per_device(basis_old, values_old, snapshots, wet_counts):
    batches, batch_width, cells = snapshots.shape
    snaps = snapshots.reshape(batches * batch_width, cells)
    far = pltpu.with_memory_space_constraint(basis_old, pltpu.HBM)
    far_snaps = pltpu.with_memory_space_constraint(snaps, pltpu.HBM)
    mine, other, near_basis, near_snaps = gram_call(wet_counts, far, far_snaps)
    mine, other = total_over_devices(mine, other)
    coeff, values = core_call(mine, other, values_old[None, :], batches)
    basis = apply_call(wet_counts, coeff, near_basis, near_snaps)
    return basis, values[0]


def solution(mesh):
    return jax.shard_map(
        per_device,
        mesh=mesh,
        in_specs=(P(None, ("grp", "dev")), P(), P(None, None, ("grp", "dev")), P(("grp", "dev"))),
        out_specs=(P(None, ("grp", "dev")), P()),
        check_vma=False,
    )
```

```python
import functools

import jax
import jax.numpy as jnp
from jax import lax
from jax.experimental import pallas as pl
from jax.experimental.pallas import tpu as pltpu
from jax.sharding import PartitionSpec as P

BLOCK = 128
SWEEPS = 3
EARLY_TILES = 3
MODES = 128
GRAM_PARTS = 8
APPLY_PARTS = 16
GRAM_VMEM = 8 << 20
CORE_VMEM = 8 << 20
APPLY_VMEM = 14 << 20
F32 = jnp.float32
BF16 = jnp.bfloat16
HIGHEST = lax.Precision.HIGHEST


def dot_nn(left_op, right_op, precision=None):
    return lax.dot_general(
        left_op, right_op, (((1,), (0,)), ((), ())), precision=precision, preferred_element_type=F32
    )


def dot_nt(left_op, right_op, precision=None):
    return lax.dot_general(
        left_op, right_op, (((1,), (1,)), ((), ())), precision=precision, preferred_element_type=F32
    )


def split_rows(basis, snap, start, wet):
    cell = lax.broadcasted_iota(jnp.int32, snap.shape, 1) + start
    snap = jnp.where(cell < wet * BLOCK, snap, 0.0)
    basis_lead, snap_lead = basis.astype(BF16), snap.astype(BF16)
    basis_rest = (basis - basis_lead.astype(F32)).astype(BF16)
    snap_rest = (snap - snap_lead.astype(F32)).astype(BF16)
    return (
        jnp.concatenate([basis_lead, snap_lead], 0),
        jnp.concatenate([basis_rest, snap_rest], 0),
    )


def gram_kernel(
    wet_ref, basis_hbm, snap_hbm, mine_ref, other_ref, basis_buf, snap_buf, arrived, even_acc, cross_acc, energy
):
    width = basis_hbm.shape[1] // GRAM_PARTS
    copies = []
    for part in range(GRAM_PARTS):
        span = pl.ds(part * width, width)
        copies.append(
            [
                pltpu.make_async_copy(source.at[:, span], target.at[:, span], arrived.at[which, part])
                for which, (source, target) in enumerate(
                    [(basis_hbm, basis_buf), (snap_hbm, snap_buf)]
                )
            ]
        )
        for copy in copies[-1]:
            copy.start()
    for part in range(GRAM_PARTS):
        for copy in copies[part]:
            copy.wait()
        span = pl.ds(part * width, width)
        lead, rest = split_rows(basis_buf[:, span], snap_buf[:, span], part * width, wet_ref[0])
        step, mixed_step = dot_nt(lead, lead), dot_nt(rest, lead)
        square = rest.astype(F32)
        square = square * square
        folded = square[:, :BLOCK]
        for k in range(1, width // BLOCK):
            folded = folded + square[:, k * BLOCK : (k + 1) * BLOCK]
        even_acc[...] = step if part == 0 else even_acc[...] + step
        cross_acc[...] = mixed_step if part == 0 else cross_acc[...] + mixed_step
        energy[...] = folded if part == 0 else energy[...] + folded

    row = lax.broadcasted_iota(jnp.int32, (MODES, MODES), 0)
    lane = lax.broadcasted_iota(jnp.int32, (MODES, MODES), 1)
    cross = cross_acc[...]
    gram = even_acc[...] + (cross + cross.T)
    extra_basis = jnp.sum(energy[:MODES, :], 1, keepdims=True)
    extra_snap = jnp.sum(energy[MODES:, :], 1, keepdims=True)
    basis_gram = gram[:MODES, :MODES] + jnp.where(row == lane, extra_basis, 0.0)
    snap_gram = gram[MODES:, MODES:]
    diagonal = jnp.sum(jnp.where(row == lane, snap_gram + extra_snap, 0.0), 0, keepdims=True)
    extra = jnp.where(
        lax.broadcasted_iota(jnp.int32, (8, MODES), 0) == 0,
        jnp.broadcast_to(diagonal, (8, MODES)),
        jnp.full((8, MODES), wet_ref[0].astype(F32)),
    )
    symmetric = jnp.concatenate([jnp.where(lane <= row, basis_gram, snap_gram), extra], 0)
    mixed = jnp.concatenate([gram[:MODES, MODES:], jnp.zeros((8, MODES), F32)], 0)
    first = lax.axis_index("grp") % 2 == 0
    mine_ref[...] = jnp.where(first, symmetric, mixed)
    other_ref[...] = jnp.where(first, mixed, symmetric)


def lane_of(tile, index):
    return jnp.broadcast_to(tile[:, index : index + 1], tile.shape)


def row_of(tile, index):
    return jnp.broadcast_to(tile[index : index + 1, :], tile.shape)


def tree_sum(terms):
    while len(terms) > 1:
        terms = [
            terms[i] + terms[i + 1] if i + 1 < len(terms) else terms[i]
            for i in range(0, len(terms), 2)
        ]
    return terms[0]


def factor_steps(tiles, base, never):
    sub = lax.broadcasted_iota(jnp.int32, (8, MODES), 0)
    lane = lax.broadcasted_iota(jnp.int32, (8, MODES), 1)
    tiles = list(tiles)
    finished = []
    for block in range(len(tiles)):
        start = base + 8 * block
        tile = tiles[block]
        cols = [lane_of(tile, start + j) for j in range(8)]
        early = {}
        for other in range(block + 1, min(len(tiles), block + 1 + EARLY_TILES)):
            early[other] = [lane_of(tiles[other], start + c) for c in range(8)]
            cols = [jnp.where(never, e, c) for e, c in zip(early[other], cols)]
        pivot = row_of(cols[0], 0)
        pivots = pivot
        for k in range(8):
            unit = jnp.where(sub == k, 1.0, 0.0)
            if k < 7:
                inverse = 1.0 / pivot
                scale = jnp.where(sub > k, cols[k], 0.0) * inverse
                pivot = row_of(cols[k + 1], k + 1) - (row_of(cols[k], k + 1) * inverse) * row_of(
                    cols[k + 1], k
                )
                pivots = jnp.where(sub > k, pivot, pivots)
                for j in range(8):
                    if j != k:
                        cols[j] = cols[j] - scale * row_of(cols[j], k)
                cols[k] = unit - scale
            else:
                cols[k] = unit
        root = lax.rsqrt(pivots)
        cols = [c * root for c in cols]
        inside = (lane >= start) & (lane < start + 8)
        tile = jnp.where(inside, jnp.where(lane - start == sub, 1.0, 0.0), tile)
        done = tree_sum([cols[c] * row_of(tile, c) for c in range(8)])
        finished.append(jnp.where(lane < start + 8, done, 0.0))
        yield
        if block + 1 == len(tiles):
            break
        done_rows = [row_of(done, r) for r in range(8)]
        update = [
            tree_sum([row_of(cols[c], r) * done_rows[r] for r in range(c, 8)]) for c in range(8)
        ]
        for other in range(block + 1, len(tiles)):
            kept = jnp.where(inside, 0.0, tiles[other])
            if other in early:
                across = early[other]
            else:
                across = [lane_of(tiles[other], start + c) for c in range(8)]
            tiles[other] = kept - tree_sum([across[c] * update[c] for c in range(8)])
    return finished


def run_together(*steppers):
    results = [None] * len(steppers)
    open_ones = dict(enumerate(steppers))
    while open_ones:
        for which, stepper in list(open_ones.items()):
            try:
                next(stepper)
            except StopIteration as end:
                results[which] = end.value
                del open_ones[which]
    return results


def tiles_of(matrix, start, count):
    return [matrix[start + 8 * i : start + 8 * i + 8] for i in range(count)]


def core_kernel(batches, mine_ref, other_ref, values_ref, coeff_ref, out_ref, frame):
    first = lax.axis_index("grp") % 2 == 0
    mine, other = mine_ref[...], other_ref[...]
    symmetric = jnp.where(first, mine, other)
    mixed = jnp.where(first, other, mine)[:MODES]
    row = lax.broadcasted_iota(jnp.int32, (MODES, MODES), 0)
    lane = lax.broadcasted_iota(jnp.int32, (MODES, MODES), 1)
    identity = jnp.where(row == lane, 1.0, 0.0)
    wet_total = symmetric[MODES + 1 : MODES + 2, 0:1] * BLOCK
    weight = 1.0 / wet_total
    never = jnp.broadcast_to(wet_total, (8, MODES)) < 0.0
    diagonal = symmetric[MODES : MODES + 1, :] * weight
    symmetric = symmetric[:MODES] * weight
    flipped = symmetric.T
    basis_gram = jnp.where(lane <= row, symmetric, flipped)
    snap_gram = jnp.where(lane > row, symmetric, jnp.where(lane == row, diagonal, flipped))
    mixed = mixed * weight
    gram_all = jnp.concatenate(
        [
            jnp.concatenate([basis_gram, mixed], 1),
            jnp.concatenate([mixed.T, snap_gram], 1),
        ],
        0,
    )
    coeff = jnp.concatenate([identity, jnp.zeros((MODES, MODES), F32)], 1)
    squares = values_ref[...] * values_ref[...]
    width = MODES // batches
    for batch in range(batches):
        chosen = (lane >= batch * width) & (lane < (batch + 1) * width)
        if batch == 0:
            project = jnp.where(chosen, mixed, 0.0)
        else:
            project = jnp.where(chosen, dot_nn(coeff, gram_all[:, MODES:], HIGHEST), 0.0)
        project_t = project.T
        own = jnp.where(chosen, identity, 0.0)
        remainder = (
            jnp.concatenate([jnp.zeros((MODES, MODES), F32), own], 1)
            - dot_nn(project_t, coeff, HIGHEST)
        )
        gram = dot_nt(dot_nn(remainder, gram_all, HIGHEST), remainder, HIGHEST)
        low = batch * width
        head = jnp.where(row == lane, squares, 0.0) + dot_nn(project, project_t, HIGHEST)
        square = dot_nt(head, head, HIGHEST) + dot_nt(
            dot_nn(project, gram, HIGHEST), project, HIGHEST
        )
        tiles, inverse = run_together(
            factor_steps(tiles_of(gram, low, width // 8), low, never),
            factor_steps(tiles_of(square, 0, MODES // 8), 0, never),
        )
        blank = jnp.zeros((width, MODES), F32)
        factor_inv = jnp.concatenate(
            [blank] * batch + tiles + [blank] * (batches - 1 - batch), 0
        )
        factor_t = dot_nn(factor_inv, gram, HIGHEST)
        factor_t = jnp.where((row <= lane) & chosen, factor_t, 0.0)
        factor = factor_t.T
        fresh = dot_nn(factor_inv, remainder, HIGHEST)
        right = jnp.concatenate([project, factor_t], 0)
        right_t = jnp.concatenate([project_t, factor], 1)
        square_row = jnp.concatenate([squares, jnp.zeros((1, MODES), F32)], 1)
        grown = jnp.concatenate([head, dot_nn(project, factor, HIGHEST)], 1)
        frame[...] = dot_nn(jnp.concatenate(inverse, 0), grown, HIGHEST)

        def sweep(repeat, carry):
            now = frame[...]
            grown = now * square_row + dot_nn(dot_nn(now, right, HIGHEST), right_t, HIGHEST)
            square = dot_nt(grown, grown, HIGHEST)
            (inverse,) = run_together(factor_steps(tiles_of(square, 0, MODES // 8), 0, never))
            frame[...] = dot_nn(jnp.concatenate(inverse, 0), grown, HIGHEST)
            return carry

        lax.fori_loop(1, SWEEPS, sweep, 0)
        now = frame[...]
        side = dot_nn(now, right, HIGHEST)
        head = now[:, :MODES]
        energy = head * head * squares + side * side
        squares = dot_nt(jnp.ones((8, MODES), F32), energy, HIGHEST)[:1]
        coeff = dot_nn(now, jnp.concatenate([coeff, fresh], 0), HIGHEST)
    lead = coeff.astype(BF16)
    rest = (coeff - lead.astype(F32)).astype(BF16)
    coeff_ref[...] = jnp.concatenate([lead, rest], 0)
    out_ref[...] = jnp.sqrt(squares)


def apply_kernel(wet_ref, coeff_ref, basis_ref, snap_ref, out_hbm, buffer, sent):
    width = out_hbm.shape[1] // APPLY_PARTS
    copies = []
    for part in range(APPLY_PARTS):
        span = pl.ds(part * width, width)
        lead, rest = split_rows(basis_ref[:, span], snap_ref[:, span], part * width, wet_ref[0])
        both = dot_nn(coeff_ref[...], lead)
        buffer[:, span] = (both[:MODES] + both[MODES:]) + dot_nn(coeff_ref[:MODES, :], rest)
        copies.append(
            pltpu.make_async_copy(buffer.at[:, span], out_hbm.at[:, span], sent.at[part])
        )
        copies[-1].start()
    for copy in copies:
        copy.wait()


def exchange(array, axis, move):
    size = lax.axis_size(axis)
    return lax.ppermute(array, axis, [(i, move(i)) for i in range(size)])


def ring_step(axis, stride, hop):
    def move(i):
        place = (i // stride) % 4
        return i + ((place + hop) % 4 - place) * stride

    return functools.partial(exchange, axis=axis, move=move)


def total_over_devices(mine, other):
    part = mine + exchange(other, "grp", lambda i: i ^ 1)
    for axis, stride in (("grp", 2), ("dev", 1), ("dev", 4)):
        part = (part + ring_step(axis, stride, 2)(part)) + (
            ring_step(axis, stride, 1)(part) + ring_step(axis, stride, 3)(part)
        )
    return part, exchange(part, "grp", lambda i: i ^ 1)


VMEM = pl.BlockSpec(memory_space=pltpu.VMEM)
SMEM = pl.BlockSpec(memory_space=pltpu.SMEM)
ANYWHERE = pl.BlockSpec(memory_space=pl.ANY)


def gram_call(wet, basis, snaps):
    cells = basis.shape[1]
    half = jax.ShapeDtypeStruct((MODES + 8, MODES), F32)
    near = jax.ShapeDtypeStruct((MODES, cells), F32)
    return pl.pallas_call(
        gram_kernel,
        in_specs=[SMEM, ANYWHERE, ANYWHERE],
        out_specs=[VMEM] * 4,
        out_shape=[half, half, near, near],
        scratch_shapes=[
            pltpu.SemaphoreType.DMA((2, GRAM_PARTS)),
            pltpu.VMEM((2 * MODES, 2 * MODES), F32),
            pltpu.VMEM((2 * MODES, 2 * MODES), F32),
            pltpu.VMEM((2 * MODES, BLOCK), F32),
        ],
        compiler_params=pltpu.CompilerParams(vmem_limit_bytes=GRAM_VMEM),
        name="gram",
    )(wet, basis, snaps)


def core_call(mine, other, values, batches=2):
    return pl.pallas_call(
        functools.partial(core_kernel, batches),
        in_specs=[VMEM, VMEM, VMEM],
        out_specs=[VMEM, VMEM],
        out_shape=[
            jax.ShapeDtypeStruct((2 * MODES, 2 * MODES), BF16),
            jax.ShapeDtypeStruct((1, MODES), F32),
        ],
        scratch_shapes=[pltpu.VMEM((MODES, 2 * MODES), F32)],
        compiler_params=pltpu.CompilerParams(vmem_limit_bytes=CORE_VMEM),
        name="core",
    )(mine, other, values)


def apply_call(wet, coeff, basis, snaps):
    cells = basis.shape[1]
    return pl.pallas_call(
        apply_kernel,
        in_specs=[SMEM, VMEM, VMEM, VMEM],
        out_specs=ANYWHERE,
        out_shape=jax.ShapeDtypeStruct((MODES, cells), F32),
        scratch_shapes=[
            pltpu.VMEM((MODES, cells), F32),
            pltpu.SemaphoreType.DMA((APPLY_PARTS,)),
        ],
        compiler_params=pltpu.CompilerParams(vmem_limit_bytes=APPLY_VMEM),
        name="apply",
    )(wet, coeff, basis, snaps)


def per_device(basis_old, values_old, snapshots, wet_counts):
    batches, batch_width, cells = snapshots.shape
    snaps = snapshots.reshape(batches * batch_width, cells)
    far = pltpu.with_memory_space_constraint(basis_old, pltpu.HBM)
    far_snaps = pltpu.with_memory_space_constraint(snaps, pltpu.HBM)
    mine, other, near_basis, near_snaps = gram_call(wet_counts, far, far_snaps)
    mine, other = total_over_devices(mine, other)
    coeff, values = core_call(mine, other, values_old[None, :], batches)
    basis = apply_call(wet_counts, coeff, near_basis, near_snaps)
    return basis, values[0]


def solution(mesh):
    return jax.shard_map(
        per_device,
        mesh=mesh,
        in_specs=(P(None, ("grp", "dev")), P(), P(None, None, ("grp", "dev")), P(("grp", "dev"))),
        out_specs=(P(None, ("grp", "dev")), P()),
        check_vma=False,
    )
```

```python
import functools

import jax
import jax.numpy as jnp
from jax import lax
from jax.experimental import pallas as pl
from jax.experimental.pallas import tpu as pltpu
from jax.sharding import PartitionSpec as P

BLOCK = 128
SWEEPS = 3
EARLY_TILES = 3
MODES = 128
GRAM_PARTS = 4
APPLY_PARTS = 16
GRAM_VMEM = 8 << 20
CORE_VMEM = 8 << 20
APPLY_VMEM = 14 << 20
F32 = jnp.float32
BF16 = jnp.bfloat16
HIGHEST = lax.Precision.HIGHEST


def dot_nn(left_op, right_op, precision=None):
    return lax.dot_general(
        left_op, right_op, (((1,), (0,)), ((), ())), precision=precision, preferred_element_type=F32
    )


def dot_nt(left_op, right_op, precision=None):
    return lax.dot_general(
        left_op, right_op, (((1,), (1,)), ((), ())), precision=precision, preferred_element_type=F32
    )


def split_rows(basis, snap, start, wet):
    cell = lax.broadcasted_iota(jnp.int32, snap.shape, 1) + start
    snap = jnp.where(cell < wet * BLOCK, snap, 0.0)
    basis_lead, snap_lead = basis.astype(BF16), snap.astype(BF16)
    basis_rest = (basis - basis_lead.astype(F32)).astype(BF16)
    snap_rest = (snap - snap_lead.astype(F32)).astype(BF16)
    return (
        jnp.concatenate([basis_lead, snap_lead], 0),
        jnp.concatenate([basis_rest, snap_rest], 0),
    )


def gram_kernel(
    wet_ref, basis_hbm, snap_hbm, mine_ref, other_ref, basis_buf, snap_buf, arrived, even_acc, cross_acc, energy
):
    width = basis_hbm.shape[1] // GRAM_PARTS
    copies = []
    for part in range(GRAM_PARTS):
        span = pl.ds(part * width, width)
        copies.append(
            [
                pltpu.make_async_copy(source.at[:, span], target.at[:, span], arrived.at[which, part])
                for which, (source, target) in enumerate(
                    [(basis_hbm, basis_buf), (snap_hbm, snap_buf)]
                )
            ]
        )
        for copy in copies[-1]:
            copy.start()
    for part in range(GRAM_PARTS):
        for copy in copies[part]:
            copy.wait()
        span = pl.ds(part * width, width)
        lead, rest = split_rows(basis_buf[:, span], snap_buf[:, span], part * width, wet_ref[0])
        step, mixed_step = dot_nt(lead, lead), dot_nt(rest, lead)
        square = rest.astype(F32)
        square = square * square
        folded = square[:, :BLOCK]
        for k in range(1, width // BLOCK):
            folded = folded + square[:, k * BLOCK : (k + 1) * BLOCK]
        even_acc[...] = step if part == 0 else even_acc[...] + step
        cross_acc[...] = mixed_step if part == 0 else cross_acc[...] + mixed_step
        energy[...] = folded if part == 0 else energy[...] + folded

    row = lax.broadcasted_iota(jnp.int32, (MODES, MODES), 0)
    lane = lax.broadcasted_iota(jnp.int32, (MODES, MODES), 1)
    cross = cross_acc[...]
    gram = even_acc[...] + (cross + cross.T)
    extra_basis = jnp.sum(energy[:MODES, :], 1, keepdims=True)
    extra_snap = jnp.sum(energy[MODES:, :], 1, keepdims=True)
    basis_gram = gram[:MODES, :MODES] + jnp.where(row == lane, extra_basis, 0.0)
    snap_gram = gram[MODES:, MODES:]
    diagonal = jnp.sum(jnp.where(row == lane, snap_gram + extra_snap, 0.0), 0, keepdims=True)
    extra = jnp.where(
        lax.broadcasted_iota(jnp.int32, (8, MODES), 0) == 0,
        jnp.broadcast_to(diagonal, (8, MODES)),
        jnp.full((8, MODES), wet_ref[0].astype(F32)),
    )
    symmetric = jnp.concatenate([jnp.where(lane <= row, basis_gram, snap_gram), extra], 0)
    mixed = jnp.concatenate([gram[:MODES, MODES:], jnp.zeros((8, MODES), F32)], 0)
    first = lax.axis_index("grp") % 2 == 0
    mine_ref[...] = jnp.where(first, symmetric, mixed)
    other_ref[...] = jnp.where(first, mixed, symmetric)


def lane_of(tile, index):
    return jnp.broadcast_to(tile[:, index : index + 1], tile.shape)


def row_of(tile, index):
    return jnp.broadcast_to(tile[index : index + 1, :], tile.shape)


def tree_sum(terms):
    while len(terms) > 1:
        terms = [
            terms[i] + terms[i + 1] if i + 1 < len(terms) else terms[i]
            for i in range(0, len(terms), 2)
        ]
    return terms[0]


def factor_steps(tiles, base, never):
    sub = lax.broadcasted_iota(jnp.int32, (8, MODES), 0)
    lane = lax.broadcasted_iota(jnp.int32, (8, MODES), 1)
    tiles = list(tiles)
    finished = []
    for block in range(len(tiles)):
        start = base + 8 * block
        tile = tiles[block]
        cols = [lane_of(tile, start + j) for j in range(8)]
        early = {}
        for other in range(block + 1, min(len(tiles), block + 1 + EARLY_TILES)):
            early[other] = [lane_of(tiles[other], start + c) for c in range(8)]
            cols = [jnp.where(never, e, c) for e, c in zip(early[other], cols)]
        pivot = row_of(cols[0], 0)
        pivots = pivot
        for k in range(8):
            unit = jnp.where(sub == k, 1.0, 0.0)
            if k < 7:
                inverse = 1.0 / pivot
                scale = jnp.where(sub > k, cols[k], 0.0) * inverse
                pivot = row_of(cols[k + 1], k + 1) - (row_of(cols[k], k + 1) * inverse) * row_of(
                    cols[k + 1], k
                )
                pivots = jnp.where(sub > k, pivot, pivots)
                for j in range(8):
                    if j != k:
                        cols[j] = cols[j] - scale * row_of(cols[j], k)
                cols[k] = unit - scale
            else:
                cols[k] = unit
        root = lax.rsqrt(pivots)
        cols = [c * root for c in cols]
        inside = (lane >= start) & (lane < start + 8)
        tile = jnp.where(inside, jnp.where(lane - start == sub, 1.0, 0.0), tile)
        done = tree_sum([cols[c] * row_of(tile, c) for c in range(8)])
        finished.append(jnp.where(lane < start + 8, done, 0.0))
        yield
        if block + 1 == len(tiles):
            break
        done_rows = [row_of(done, r) for r in range(8)]
        update = [
            tree_sum([row_of(cols[c], r) * done_rows[r] for r in range(c, 8)]) for c in range(8)
        ]
        for other in range(block + 1, len(tiles)):
            kept = jnp.where(inside, 0.0, tiles[other])
            if other in early:
                across = early[other]
            else:
                across = [lane_of(tiles[other], start + c) for c in range(8)]
            tiles[other] = kept - tree_sum([across[c] * update[c] for c in range(8)])
    return finished


def run_together(*steppers):
    results = [None] * len(steppers)
    open_ones = dict(enumerate(steppers))
    while open_ones:
        for which, stepper in list(open_ones.items()):
            try:
                next(stepper)
            except StopIteration as end:
                results[which] = end.value
                del open_ones[which]
    return results


def tiles_of(matrix, start, count):
    return [matrix[start + 8 * i : start + 8 * i + 8] for i in range(count)]


def core_kernel(batches, mine_ref, other_ref, values_ref, coeff_ref, out_ref, frame):
    first = lax.axis_index("grp") % 2 == 0
    mine, other = mine_ref[...], other_ref[...]
    symmetric = jnp.where(first, mine, other)
    mixed = jnp.where(first, other, mine)[:MODES]
    row = lax.broadcasted_iota(jnp.int32, (MODES, MODES), 0)
    lane = lax.broadcasted_iota(jnp.int32, (MODES, MODES), 1)
    identity = jnp.where(row == lane, 1.0, 0.0)
    wet_total = symmetric[MODES + 1 : MODES + 2, 0:1] * BLOCK
    weight = 1.0 / wet_total
    never = jnp.broadcast_to(wet_total, (8, MODES)) < 0.0
    diagonal = symmetric[MODES : MODES + 1, :] * weight
    symmetric = symmetric[:MODES] * weight
    flipped = symmetric.T
    basis_gram = jnp.where(lane <= row, symmetric, flipped)
    snap_gram = jnp.where(lane > row, symmetric, jnp.where(lane == row, diagonal, flipped))
    mixed = mixed * weight
    gram_all = jnp.concatenate(
        [
            jnp.concatenate([basis_gram, mixed], 1),
            jnp.concatenate([mixed.T, snap_gram], 1),
        ],
        0,
    )
    coeff = jnp.concatenate([identity, jnp.zeros((MODES, MODES), F32)], 1)
    squares = values_ref[...] * values_ref[...]
    width = MODES // batches
    for batch in range(batches):
        chosen = (lane >= batch * width) & (lane < (batch + 1) * width)
        if batch == 0:
            project = jnp.where(chosen, mixed, 0.0)
        else:
            project = jnp.where(chosen, dot_nn(coeff, gram_all[:, MODES:], HIGHEST), 0.0)
        project_t = project.T
        own = jnp.where(chosen, identity, 0.0)
        if batch == 0:
            remainder = jnp.concatenate([-project_t, own], 1)
        else:
            remainder = jnp.concatenate(
                [jnp.zeros((MODES, MODES), F32), own], 1
            ) - dot_nn(project_t, coeff, HIGHEST)
        gram = dot_nt(dot_nn(remainder, gram_all, HIGHEST), remainder, HIGHEST)
        low = batch * width
        head = jnp.where(row == lane, squares, 0.0) + dot_nn(project, project_t, HIGHEST)
        square = dot_nt(head, head, HIGHEST) + dot_nt(
            dot_nn(project, gram, HIGHEST), project, HIGHEST
        )
        tiles, inverse = run_together(
            factor_steps(tiles_of(gram, low, width // 8), low, never),
            factor_steps(tiles_of(square, 0, MODES // 8), 0, never),
        )
        blank = jnp.zeros((width, MODES), F32)
        factor_inv = jnp.concatenate(
            [blank] * batch + tiles + [blank] * (batches - 1 - batch), 0
        )
        factor_t = dot_nn(factor_inv, gram, HIGHEST)
        factor_t = jnp.where((row <= lane) & chosen, factor_t, 0.0)
        factor = factor_t.T
        fresh = dot_nn(factor_inv, remainder, HIGHEST)
        right = jnp.concatenate([project, factor_t], 0)
        right_t = jnp.concatenate([project_t, factor], 1)
        square_row = jnp.concatenate([squares, jnp.zeros((1, MODES), F32)], 1)
        grown = jnp.concatenate([head, dot_nn(project, factor, HIGHEST)], 1)
        frame[...] = dot_nn(jnp.concatenate(inverse, 0), grown, HIGHEST)

        def sweep(repeat, carry):
            now = frame[...]
            grown = now * square_row + dot_nn(dot_nn(now, right, HIGHEST), right_t, HIGHEST)
            square = dot_nt(grown, grown, HIGHEST)
            (inverse,) = run_together(factor_steps(tiles_of(square, 0, MODES // 8), 0, never))
            frame[...] = dot_nn(jnp.concatenate(inverse, 0), grown, HIGHEST)
            return carry

        lax.fori_loop(1, SWEEPS, sweep, 0)
        now = frame[...]
        side = dot_nn(now, right, HIGHEST)
        head = now[:, :MODES]
        energy = head * head * squares + side * side
        squares = dot_nt(jnp.ones((8, MODES), F32), energy, HIGHEST)[:1]
        coeff = dot_nn(now, jnp.concatenate([coeff, fresh], 0), HIGHEST)
    lead = coeff.astype(BF16)
    rest = (coeff - lead.astype(F32)).astype(BF16)
    coeff_ref[...] = jnp.concatenate([lead, rest], 0)
    out_ref[...] = jnp.sqrt(squares)


def apply_kernel(wet_ref, coeff_ref, basis_ref, snap_ref, out_hbm, buffer, sent):
    width = out_hbm.shape[1] // APPLY_PARTS
    copies = []
    for part in range(APPLY_PARTS):
        span = pl.ds(part * width, width)
        lead, rest = split_rows(basis_ref[:, span], snap_ref[:, span], part * width, wet_ref[0])
        both = dot_nn(coeff_ref[...], lead)
        buffer[:, span] = (both[:MODES] + both[MODES:]) + dot_nn(coeff_ref[:MODES, :], rest)
        copies.append(
            pltpu.make_async_copy(buffer.at[:, span], out_hbm.at[:, span], sent.at[part])
        )
        copies[-1].start()
    for copy in copies:
        copy.wait()


def exchange(array, axis, move):
    size = lax.axis_size(axis)
    return lax.ppermute(array, axis, [(i, move(i)) for i in range(size)])


def ring_step(axis, stride, hop):
    def move(i):
        place = (i // stride) % 4
        return i + ((place + hop) % 4 - place) * stride

    return functools.partial(exchange, axis=axis, move=move)


def total_over_devices(mine, other):
    part = mine + exchange(other, "grp", lambda i: i ^ 1)
    for axis, stride in (("grp", 2), ("dev", 1), ("dev", 4)):
        part = (part + ring_step(axis, stride, 2)(part)) + (
            ring_step(axis, stride, 1)(part) + ring_step(axis, stride, 3)(part)
        )
    return part, exchange(part, "grp", lambda i: i ^ 1)


VMEM = pl.BlockSpec(memory_space=pltpu.VMEM)
SMEM = pl.BlockSpec(memory_space=pltpu.SMEM)
ANYWHERE = pl.BlockSpec(memory_space=pl.ANY)


def gram_call(wet, basis, snaps):
    cells = basis.shape[1]
    half = jax.ShapeDtypeStruct((MODES + 8, MODES), F32)
    near = jax.ShapeDtypeStruct((MODES, cells), F32)
    return pl.pallas_call(
        gram_kernel,
        in_specs=[SMEM, ANYWHERE, ANYWHERE],
        out_specs=[VMEM] * 4,
        out_shape=[half, half, near, near],
        scratch_shapes=[
            pltpu.SemaphoreType.DMA((2, GRAM_PARTS)),
            pltpu.VMEM((2 * MODES, 2 * MODES), F32),
            pltpu.VMEM((2 * MODES, 2 * MODES), F32),
            pltpu.VMEM((2 * MODES, BLOCK), F32),
        ],
        compiler_params=pltpu.CompilerParams(vmem_limit_bytes=GRAM_VMEM),
        name="gram",
    )(wet, basis, snaps)


def core_call(mine, other, values, batches=2):
    return pl.pallas_call(
        functools.partial(core_kernel, batches),
        in_specs=[VMEM, VMEM, VMEM],
        out_specs=[VMEM, VMEM],
        out_shape=[
            jax.ShapeDtypeStruct((2 * MODES, 2 * MODES), BF16),
            jax.ShapeDtypeStruct((1, MODES), F32),
        ],
        scratch_shapes=[pltpu.VMEM((MODES, 2 * MODES), F32)],
        compiler_params=pltpu.CompilerParams(vmem_limit_bytes=CORE_VMEM),
        name="core",
    )(mine, other, values)


def apply_call(wet, coeff, basis, snaps):
    cells = basis.shape[1]
    return pl.pallas_call(
        apply_kernel,
        in_specs=[SMEM, VMEM, VMEM, VMEM],
        out_specs=ANYWHERE,
        out_shape=jax.ShapeDtypeStruct((MODES, cells), F32),
        scratch_shapes=[
            pltpu.VMEM((MODES, cells), F32),
            pltpu.SemaphoreType.DMA((APPLY_PARTS,)),
        ],
        compiler_params=pltpu.CompilerParams(vmem_limit_bytes=APPLY_VMEM),
        name="apply",
    )(wet, coeff, basis, snaps)


def per_device(basis_old, values_old, snapshots, wet_counts):
    batches, batch_width, cells = snapshots.shape
    snaps = snapshots.reshape(batches * batch_width, cells)
    far = pltpu.with_memory_space_constraint(basis_old, pltpu.HBM)
    far_snaps = pltpu.with_memory_space_constraint(snaps, pltpu.HBM)
    mine, other, near_basis, near_snaps = gram_call(wet_counts, far, far_snaps)
    mine, other = total_over_devices(mine, other)
    coeff, values = core_call(mine, other, values_old[None, :], batches)
    basis = apply_call(wet_counts, coeff, near_basis, near_snaps)
    return basis, values[0]


def solution(mesh):
    return jax.shard_map(
        per_device,
        mesh=mesh,
        in_specs=(P(None, ("grp", "dev")), P(), P(None, None, ("grp", "dev")), P(("grp", "dev"))),
        out_specs=(P(None, ("grp", "dev")), P()),
        check_vma=False,
    )
```
